32 devices in a mesh: real: 2 (over y), rows: 4 (over z), orb: 4 (over x, core).
Axes of the slice: x: 2, y: 2, z: 4, core: 2. Of those that a mesh axis runs over, the one named last changes fastest.
Arguments:
- occupied: bfloat16 [2, 16, 256, 1024], P(None, ('real', 'rows'), None, 'orb'), parts along dimension 1, may hold values from -2.5 to 2.5
- disorder: int32 [16, 256], P(('real', 'rows')), parts along dimension 0, may hold values from -8 to 8
- region_cols: int32 [32], replicated, may hold values from 0 to 255, as said below
- cheb_coef: float32 [2, 8], replicated, may hold values from -0.6 to 0.6
- prior_corr: bfloat16 [2, 512, 256], P(None, ('real', 'rows'), 'orb'), parts along dimension 1, may hold values from -6 to 6
Outputs:
- correlation: float32 [2, 512, 256], P(None, ('real', 'rows'), 'orb'), parts along dimension 1
The draws below stay inside these ranges and needn't reach their ends.
There are 2 independent parts, one for each index of `real`. The reference program is written for one: setup_inputs(seed, part) draws one part's arguments, and reference() takes and returns one part's arrays. A program takes and returns all parts, laid end to end along the dimension named above; an argument that names none is the same for every part. Nothing has to cross between parts.
Inputs may be any that keep to these rules, and one draw needn't show every extreme that they name: `region_cols`: 32 distinct columns; columns 0 and 255 are always among them.
All inputs are finite; a program needn't handle non-finite values.
Results may differ from the reference program's by a relative error of at most 0.0033.
Values may be sent and summed in bfloat16 or wider, within the bound.
A program may use at most 64 MiB of HBM per device.

```python
import jax
import jax.numpy as jnp
from jax import lax

LX = 256
M = 1024
ACOLS = 32
KTERMS = 8
LY = 8
NA = 256


def draw_region_cols(key, part):
    inner = jax.random.permutation(jax.random.fold_in(key, 11), LX - 2)[:ACOLS - 2] + 1
    columns = jnp.concatenate([jnp.array([0, LX - 1], jnp.int32), inner.astype(jnp.int32)])
    shuffle = jax.random.permutation(jax.random.fold_in(key, 12), ACOLS)
    return columns[shuffle]


def place_ends(drawn, key, low, largest):
    dims = drawn.shape
    place = [jax.random.randint(jax.random.fold_in(key, axis), (), 0, dims[axis]) for axis in range(len(dims))]
    drawn = drawn.at[tuple(place)].set(low)
    longest = dims.index(max(dims))
    place[longest] = (place[longest] + 1) % dims[longest]
    return drawn.at[tuple(place)].set(largest)


def level_of(rng, dims, pieces, smallest, high):
    def one(dim, blocks):
        steps = jax.random.uniform(jax.random.fold_in(jax.random.fold_in(rng, 6), dim), (blocks,), jnp.float32, smallest / len(pieces), high / len(pieces))
        return jnp.repeat(jnp.exp(steps), dims[dim] // blocks).reshape((-1,) + (1,) * (len(dims) - dim - 1))

    loudness = one(*pieces[0])
    for cut in pieces[1:]:
        loudness = loudness * one(*cut)
    return loudness


def centred(key, extent, width, most, shards=(), kind=jnp.bfloat16):
    drawn = width * jax.random.normal(key, extent, jnp.float32)
    if shards:
        drawn = drawn * level_of(key, extent, shards, -0.22, 0.18)
    return jnp.clip(drawn, -most, most).astype(kind)


def setup_inputs(seed: int = 0, part: int = 0) -> dict:
    key_list = jax.random.split(jax.random.key(seed), 6)
    own_keys = jax.random.split(jax.random.fold_in(key_list[5], part), 6)
    occupied = centred(own_keys[0], (2, LY, LX, M), 0.18, 2.5, ((1, 4), (3, 4)))
    disorder = place_ends(jax.random.randint(own_keys[1], (LY, LX), -8, 9), jax.random.fold_in(own_keys[1], 1), -8, 8).astype(jnp.int32)
    region_cols = draw_region_cols(jax.random.fold_in(key_list[5], 71), part)
    cheb_coef = jnp.clip(jax.random.uniform(key_list[3], (2, KTERMS), jnp.float32, -0.6, 0.6), -0.6, 0.6)
    prior_corr = centred(own_keys[4], (2, NA, NA), 1.0, 6.0, ((1, 4), (2, 4)))
    return {"occupied": occupied, "disorder": disorder, "region_cols": region_cols, "cheb_coef": cheb_coef, "prior_corr": prior_corr}


HOP_SCALE = 5.25
LEVEL_STEP = 0.125


def apply_hop(state, onsite):
    neighbours = jnp.roll(state, -1, 1) + jnp.roll(state, 1, 1) + jnp.roll(state, -1, 2) + jnp.roll(state, 1, 2)
    return (onsite[None, :, :, None] * state - neighbours) / HOP_SCALE


def rotate(picked):
    return jnp.stack([-picked[1], picked[0]])


def reference(occupied, disorder, region_cols, cheb_coef, prior_corr):
    onsite = disorder.astype(jnp.float32) * LEVEL_STEP
    current = occupied.astype(jnp.float32)

    def select_cols(state):
        return jnp.take(state, region_cols, axis=2)

    picked = select_cols(current)
    summed = cheb_coef[0, 0] * picked + cheb_coef[1, 0] * rotate(picked)
    previous = current
    for degree in range(1, KTERMS):
        applied = apply_hop(current, onsite)
        following = applied if degree == 1 else 2.0 * applied - previous
        previous, current = current, following
        picked = select_cols(current)
        summed = summed + (cheb_coef[0, degree] * picked + cheb_coef[1, degree] * rotate(picked))
    evolved = summed.astype(jnp.bfloat16).reshape(2, LY * ACOLS, M)
    evolved_wide = evolved.astype(jnp.float32)
    block_rows = 8 * ACOLS

    def row_block(index):
        part = lax.dynamic_slice_in_dim(evolved_wide, index * block_rows, block_rows, 1)
        products = jnp.einsum("cim,djm->cdij", part, evolved_wide)
        return jnp.stack([products[0, 0] + products[1, 1], products[1, 0] - products[0, 1]])

    blocks = lax.map(row_block, jnp.arange(LY // 8, dtype=jnp.int32))
    tiles = jnp.transpose(blocks, (1, 0, 2, 3)).reshape(2, LY * ACOLS, LY * ACOLS)
    return prior_corr.astype(jnp.float32) + tiles
```

```python
import functools

import jax
import jax.numpy as jnp
from jax import lax
from jax.experimental import pallas as pl
from jax.experimental.pallas import tpu as pltpu
from jax.sharding import PartitionSpec as P

HOP_SCALE = 5.25
LEVEL_STEP = 0.125


def padded_2(cells, sides, width):
    for axis, dim in sides:
        count = lax.axis_size(axis)
        head = lax.slice_in_dim(cells, 0, width, axis=dim)
        tail = lax.slice_in_dim(cells, cells.shape[dim] - width, cells.shape[dim], axis=dim)
        cells = jnp.concatenate(
            [
                lax.ppermute(tail, axis, [(i, (i + 1) % count) for i in range(count)]),
                cells,
                lax.ppermute(head, axis, [((i + 1) % count, i) for i in range(count)]),
            ],
            axis=dim,
        )
    return cells


def apply_rows(padded, onsite):
    middle = padded[:, 1:-1]
    neighbours = padded[:, 2:] + padded[:, :-2] + jnp.roll(middle, -1, 2) + jnp.roll(middle, 1, 2)
    return (onsite[None, :, :, None] * middle - neighbours) / HOP_SCALE


def rotate(picked):
    return jnp.stack([-picked[1], picked[0]])


def combine_pairs(products):
    return jnp.stack([products[0, 0] + products[1, 1], products[1, 0] - products[0, 1]])


def shards(occupied, disorder, region_cols, cheb_coef, prior_corr):
    band_rows = occupied.shape[1]
    term_count = cheb_coef.shape[1]
    current = occupied.astype(jnp.float32)

    def contribution(state, degree):
        picked = jnp.take(state, region_cols, axis=2)
        return cheb_coef[0, degree] * picked + cheb_coef[1, degree] * rotate(picked)

    summed = contribution(current, 0)
    previous = current
    onsite = disorder.astype(jnp.float32) * LEVEL_STEP
    for degree in range(1, term_count):
        padded = padded_2(current, (("rows", 1),), 1)
        applied = apply_rows(padded, onsite)
        following = applied if degree == 1 else 2.0 * applied - previous
        previous, current = (current, following)
        summed = summed + contribution(current, degree)
    tile_rows = band_rows * region_cols.shape[0]
    evolved = summed.astype(jnp.bfloat16).reshape(2, tile_rows, summed.shape[3])
    row_panel = lax.all_gather(evolved, "orb", axis=2, tiled=True)
    column_all = lax.all_gather(evolved, "rows", axis=1, tiled=True)
    column_panel = lax.all_to_all(column_all, "orb", split_axis=1, concat_axis=2, tiled=True)
    products = jnp.einsum(
        "cim,djm->cdij", row_panel, column_panel, preferred_element_type=jnp.float32
    )
    tile_sum = combine_pairs(products)
    return prior_corr.astype(jnp.float32) + tile_sum


LANES = 128
MESH = pl.DeviceIdType.MESH


def quench_kernel(
    row_count, occupied, disorder, region_cols, cheb_coef, prior, out,
    fields, levels, window, operator, evolved, partial, outgoing, incoming,
    level_send, level_recv, field_send, field_recv, forward_send,
    half_send, half_recv, block_send, block_recv,
):
    r = lax.axis_index("rows")
    o = lax.axis_index("orb")
    g = o % 2
    x = o // 2
    mate = 2 * x + 1 - g
    band, width = disorder.shape
    height = band * row_count
    terms = cheb_coef.shape[1]
    reach = terms - 1
    acols = region_cols.shape[0]
    tile = prior.shape[1]
    chips = 2 * row_count
    mine = 2 * r + x

    def remote(src, dst, send, recv, row, orb):
        return pltpu.make_async_remote_copy(
            src_ref=src, dst_ref=dst, send_sem=send, recv_sem=recv,
            device_id={"rows": row, "orb": orb}, device_id_type=MESH,
        )

    row_id = lax.broadcasted_iota(jnp.int32, (height, width), 0)
    own = disorder[...].astype(jnp.float32) * LEVEL_STEP
    slab = jnp.zeros((height, width), jnp.float32)
    for i in range(band):
        slab = jnp.where(row_id == band * r + i, own[i : i + 1, :], slab)
    levels[r] = slab

    barrier = pltpu.get_barrier_semaphore()
    for dr in range(row_count):
        for do in range(4):
            if dr or do:
                pl.semaphore_signal(
                    barrier, inc=1,
                    device_id={"rows": (r + dr) % row_count, "orb": (o + do) % 4},
                    device_id_type=MESH,
                )
    pl.semaphore_wait(barrier, 4 * row_count - 1)

    def level_copy(k, slot):
        return remote(
            levels.at[slot], levels.at[slot], level_send.at[k - 1],
            level_recv.at[slot], (r + k) % row_count, o,
        )

    for k in range(1, row_count):
        level_copy(k, r).start()

    def field_src(h, c):
        return occupied.at[c, :, :, pl.ds(h * LANES, LANES)]

    for h in range(2):
        q = 2 * g + h

        @pl.when(q == r)
        def _():
            for c in range(2):
                pltpu.make_async_copy(
                    field_src(h, c), fields.at[c, r], field_recv.at[c, r]
                ).start()
                remote(
                    field_src(h, c), fields.at[c, r], field_send.at[h, c],
                    field_recv.at[c, r], r, mate,
                ).start()

        @pl.when(q != r)
        def _():
            for c in range(2):
                remote(
                    field_src(h, c), fields.at[c, r], field_send.at[h, c],
                    field_recv.at[c, r], q, 2 * x + c,
                ).start()

    lane = lax.broadcasted_iota(jnp.int32, (1, LANES), 1)
    cols = jnp.zeros((1, LANES), jnp.int32)
    for a in range(acols):
        cols = jnp.where(lane % acols == a, region_cols[a], cols)
    offset = lax.broadcasted_iota(jnp.int32, (width, LANES), 0) - cols + reach
    offset = jnp.where(offset < 0, offset + width, offset)
    offset = jnp.where(offset >= width, offset - width, offset)

    for k in range(1, row_count):
        level_copy(k, (r + k) % row_count).wait_recv()
    onsite = levels[0]
    for slot in range(1, row_count):
        onsite = onsite + levels[slot]
    onsite = onsite.astype(jnp.bfloat16)

    local_levels = {}
    for d in range(1, 2 * reach):
        hot = jnp.where(offset == d, 1.0, 0.0).astype(jnp.bfloat16)
        local_levels[d] = jnp.dot(onsite, hot, preferred_element_type=jnp.float32)

    site_row = lane // acols + (LANES // acols) * g
    start = jnp.where(
        lax.broadcasted_iota(jnp.int32, (height, LANES), 0) == site_row, 1.0, 0.0
    )
    previous, current = {}, {reach: start}
    real = {reach: cheb_coef[0, 0] * start}
    imag = {reach: cheb_coef[1, 0] * start}
    for degree in range(1, terms):
        following = {}
        for d in range(reach - degree, reach + degree + 1):
            total = None
            if d in current:
                here = current[d]
                total = local_levels[d] * here - (
                    pltpu.roll(here, 1, 0) + pltpu.roll(here, height - 1, 0)
                )
            for side in (d - 1, d + 1):
                if side in current:
                    there = current[side]
                    total = -there if total is None else total - there
            value = total * ((1.0 if degree == 1 else 2.0) / HOP_SCALE)
            if d in previous:
                value = value - previous[d]
            following[d] = value
            more_real = cheb_coef[0, degree] * value
            more_imag = cheb_coef[1, degree] * value
            real[d] = real[d] + more_real if d in real else more_real
            imag[d] = imag[d] + more_imag if d in imag else more_imag
        previous, current = current, following
    for d in range(2 * reach + 1):
        window[0, d] = real[d]
        window[1, d] = imag[d]

    def expand(y, carry):
        for part in range(2):
            dense = jnp.zeros((width, LANES), jnp.float32)
            for d in range(2 * reach + 1):
                dense = jnp.where(offset == d, window[part, d, pl.ds(y, 1), :], dense)
            dense = dense.T
            high = dense.astype(jnp.bfloat16)
            low = (dense - high.astype(jnp.float32)).astype(jnp.bfloat16)
            operator[0, y, pl.ds(part * LANES, LANES), :] = high
            operator[1, y, pl.ds(part * LANES, LANES), :] = low
        return carry

    lax.fori_loop(0, height, expand, 0)

    def field_wait(c, slot):
        remote(
            fields.at[c, slot], fields.at[c, slot], forward_send.at[0],
            field_recv.at[c, slot], r, mate,
        ).wait_recv()

    def forward(k):
        slot = (r + k) % row_count
        return remote(
            fields.at[g, slot], fields.at[g, slot], forward_send.at[k - 1],
            field_recv.at[g, slot], r, mate,
        )

    product = jnp.zeros((2 * LANES, 2 * LANES), jnp.float32)
    for k in range(row_count):
        slot = (r + k) % row_count
        field_wait(g, slot)
        if k:
            forward(k).start()
        field_wait(1 - g, slot)
        for i in range(band):
            both = jnp.concatenate([fields[0, slot, i], fields[1, slot, i]], axis=1)
            for piece in range(2):
                product = product + jnp.dot(
                    operator[piece, band * slot + i], both,
                    preferred_element_type=jnp.float32,
                )
    evolved[g, 0] = (product[:LANES, :LANES] - product[LANES:, LANES:]).astype(jnp.bfloat16)
    evolved[g, 1] = (product[:LANES, LANES:] + product[LANES:, :LANES]).astype(jnp.bfloat16)

    def half_copy(slot):
        return remote(
            evolved.at[slot], evolved.at[slot], half_send, half_recv, r, mate
        )

    half_copy(g).start()
    half_copy(1 - g).wait_recv()

    left = jnp.concatenate(
        [jnp.concatenate([evolved[s, 0], evolved[s, 1]], axis=1) for s in range(2)], axis=0
    )
    columns = pl.ds(pl.multiple_of(g * tile, tile), tile)
    rights = []
    for s in range(2):
        p0 = evolved[s, 0, columns, :]
        p1 = evolved[s, 1, columns, :]
        rights.append(jnp.concatenate([p0, p1], axis=1))
        rights.append(jnp.concatenate([-p1, p0], axis=1))
    right = jnp.concatenate(rights, axis=0)
    blocks = lax.dot_general(
        left, right, (((1,), (1,)), ((), ())), preferred_element_type=jnp.float32
    )
    for s in range(2):
        for row in range(row_count):
            block = blocks[row * tile : (row + 1) * tile, s * LANES : (s + 1) * LANES]
            partial[2 * row + s] = block
            outgoing[2 * row + s] = block.astype(jnp.bfloat16)

    def block_copy(k, slot):
        to = (mine + k) % chips
        return remote(
            outgoing.at[to], incoming.at[slot], block_send.at[k - 1],
            block_recv.at[slot], to // 2, 2 * (to % 2) + g,
        )

    for k in range(1, chips):
        block_copy(k, mine).start()
    total = partial[mine]
    for k in range(1, chips):
        slot = (mine + chips - k) % chips
        block_copy(k, slot).wait_recv()
        total = total + incoming[slot].astype(jnp.float32)
    out[0] = prior[0].astype(jnp.float32) + total[:, :tile]
    out[1] = prior[1].astype(jnp.float32) + total[:, tile:]

    for k in range(1, row_count):
        level_copy(k, r).wait_send()
        forward(k).wait_send()
    for h in range(2):
        for c in range(2):
            remote(
                field_src(h, c), fields.at[c, r], field_send.at[h, c],
                field_recv.at[c, r], r, mate,
            ).wait_send()
    half_copy(g).wait_send()
    for k in range(1, chips):
        block_copy(k, mine).wait_send()


def fused_step(row_count, occupied, disorder, region_cols, cheb_coef, prior_corr):
    band, width = disorder.shape
    terms = cheb_coef.shape[1]
    tile = prior_corr.shape[1]
    height = band * row_count
    chips = 2 * row_count
    dma = pltpu.SemaphoreType.DMA
    vmem = pl.BlockSpec(memory_space=pltpu.VMEM)
    smem = pl.BlockSpec(memory_space=pltpu.SMEM)
    return pl.pallas_call(
        functools.partial(quench_kernel, row_count),
        out_shape=jax.ShapeDtypeStruct(prior_corr.shape, jnp.float32),
        in_specs=[pl.BlockSpec(memory_space=pl.ANY), vmem, smem, smem, vmem],
        out_specs=vmem,
        scratch_shapes=[
            pltpu.VMEM((2, row_count, band, width, LANES), jnp.bfloat16),
            pltpu.VMEM((row_count, height, width), jnp.float32),
            pltpu.VMEM((2, 2 * terms - 1, height, LANES), jnp.float32),
            pltpu.VMEM((2, height, 2 * LANES, width), jnp.bfloat16),
            pltpu.VMEM((2, 2, LANES, LANES), jnp.bfloat16),
            pltpu.VMEM((chips, tile, LANES), jnp.float32),
            pltpu.VMEM((chips, tile, LANES), jnp.bfloat16),
            pltpu.VMEM((chips, tile, LANES), jnp.bfloat16),
            dma((row_count - 1,)),
            dma((row_count,)),
            dma((2, 2)),
            dma((2, row_count)),
            dma((row_count - 1,)),
            dma,
            dma,
            dma((chips - 1,)),
            dma((chips,)),
        ],
        compiler_params=pltpu.CompilerParams(collective_id=0, has_side_effects=True),
    )(occupied, disorder, region_cols, cheb_coef, prior_corr)


def local_step(row_count, orb_count, occupied, disorder, region_cols, cheb_coef, prior_corr):
    band, width, orbitals = occupied.shape[1:]
    terms = cheb_coef.shape[1]
    height = band * row_count
    sites = height * region_cols.shape[0]
    fused = (
        orb_count == 4
        and sites == 2 * LANES
        and 2 * orbitals == row_count * LANES
        and orbitals == 2 * LANES
        and height % 8 == 0
        and width % LANES == 0
        and width >= 2 * terms
        and LANES % region_cols.shape[0] == 0
        and prior_corr.shape[1:] == (LANES // 2, LANES // 2)
    )
    if fused:
        return fused_step(row_count, occupied, disorder, region_cols, cheb_coef, prior_corr)
    return shards(occupied, disorder, region_cols, cheb_coef, prior_corr)


def solution(mesh):
    return jax.shard_map(
        functools.partial(local_step, mesh.shape["rows"], mesh.shape["orb"]),
        mesh=mesh,
        in_specs=(
            P(None, ("real", "rows"), None, "orb"),
            P(("real", "rows"), None),
            P(),
            P(),
            P(None, ("real", "rows"), "orb"),
        ),
        out_specs=P(None, ("real", "rows"), "orb"),
        check_vma=False,
    )
```

```python
import functools

import jax
import jax.numpy as jnp
from jax import lax
from jax.experimental import pallas as pl
from jax.experimental.pallas import tpu as pltpu
from jax.sharding import PartitionSpec as P

HOP_SCALE = 5.25
LEVEL_STEP = 0.125


def padded_2(cells, sides, width):
    for axis, dim in sides:
        count = lax.axis_size(axis)
        head = lax.slice_in_dim(cells, 0, width, axis=dim)
        tail = lax.slice_in_dim(cells, cells.shape[dim] - width, cells.shape[dim], axis=dim)
        cells = jnp.concatenate(
            [
                lax.ppermute(tail, axis, [(i, (i + 1) % count) for i in range(count)]),
                cells,
                lax.ppermute(head, axis, [((i + 1) % count, i) for i in range(count)]),
            ],
            axis=dim,
        )
    return cells


def apply_rows(padded, onsite):
    middle = padded[:, 1:-1]
    neighbours = padded[:, 2:] + padded[:, :-2] + jnp.roll(middle, -1, 2) + jnp.roll(middle, 1, 2)
    return (onsite[None, :, :, None] * middle - neighbours) / HOP_SCALE


def rotate(picked):
    return jnp.stack([-picked[1], picked[0]])


def combine_pairs(products):
    return jnp.stack([products[0, 0] + products[1, 1], products[1, 0] - products[0, 1]])


def shards(occupied, disorder, region_cols, cheb_coef, prior_corr):
    band_rows = occupied.shape[1]
    term_count = cheb_coef.shape[1]
    current = occupied.astype(jnp.float32)

    def contribution(state, degree):
        picked = jnp.take(state, region_cols, axis=2)
        return cheb_coef[0, degree] * picked + cheb_coef[1, degree] * rotate(picked)

    summed = contribution(current, 0)
    previous = current
    onsite = disorder.astype(jnp.float32) * LEVEL_STEP
    for degree in range(1, term_count):
        padded = padded_2(current, (("rows", 1),), 1)
        applied = apply_rows(padded, onsite)
        following = applied if degree == 1 else 2.0 * applied - previous
        previous, current = (current, following)
        summed = summed + contribution(current, degree)
    tile_rows = band_rows * region_cols.shape[0]
    evolved = summed.astype(jnp.bfloat16).reshape(2, tile_rows, summed.shape[3])
    row_panel = lax.all_gather(evolved, "orb", axis=2, tiled=True)
    column_all = lax.all_gather(evolved, "rows", axis=1, tiled=True)
    column_panel = lax.all_to_all(column_all, "orb", split_axis=1, concat_axis=2, tiled=True)
    products = jnp.einsum(
        "cim,djm->cdij", row_panel, column_panel, preferred_element_type=jnp.float32
    )
    tile_sum = combine_pairs(products)
    return prior_corr.astype(jnp.float32) + tile_sum


LANES = 128
MESH = pl.DeviceIdType.MESH


def quench_kernel(
    row_count, occupied, disorder, region_cols, cheb_coef, prior, out,
    fields, levels, hot, window, operator, product, shares, rounded, base, crossed,
    evolved, partial, outgoing, incoming,
    level_send, level_recv, field_send, field_recv, base_send, base_recv,
    cross_send, cross_recv, half_send, half_recv, block_send, block_recv,
):
    r = lax.axis_index("rows")
    o = lax.axis_index("orb")
    g = o % 2
    x = o // 2
    mate = 2 * x + 1 - g
    band, width = disorder.shape
    height = band * row_count
    terms = cheb_coef.shape[1]
    reach = terms - 1
    acols = region_cols.shape[0]
    tile = prior.shape[1]
    chips = 2 * row_count
    mine = 2 * r + x
    half = row_count // 2
    side = r // half
    place = r % half
    pair = r + 1 - 2 * place
    across = (r + half) % row_count
    owner = g == side

    def remote(src, dst, send, recv, row, orb):
        return pltpu.make_async_remote_copy(
            src_ref=src, dst_ref=dst, send_sem=send, recv_sem=recv,
            device_id={"rows": row, "orb": orb}, device_id_type=MESH,
        )

    row_id = lax.broadcasted_iota(jnp.int32, (height, width), 0)
    own = disorder[...].astype(jnp.float32) * LEVEL_STEP
    slab = jnp.zeros((height, width), jnp.float32)
    for i in range(band):
        slab = jnp.where(row_id == band * r + i, own[i : i + 1, :], slab)
    levels[r] = slab

    barrier = pltpu.get_barrier_semaphore()

    def greet(row, orb):
        pl.semaphore_signal(
            barrier, inc=1, device_id={"rows": row, "orb": orb}, device_id_type=MESH
        )

    has_left, has_right = r > 0, r < row_count - 1
    greet(r, mate)
    greet(r, (o + 2) % 4)
    pl.when(has_left)(lambda: greet((r + row_count - 1) % row_count, o))
    pl.when(has_right)(lambda: greet((r + 1) % row_count, o))
    pl.semaphore_wait(
        barrier, 2 + jnp.where(has_left, 1, 0) + jnp.where(has_right, 1, 0)
    )

    def level_copy(slot, way):
        return remote(
            levels.at[slot], levels.at[slot], level_send.at[(way + 1) // 2, slot],
            level_recv.at[slot], (r + row_count + way) % row_count, o,
        )

    pl.when(has_left)(lambda: level_copy(r, -1).start())
    pl.when(has_right)(lambda: level_copy(r, 1).start())

    def chunk(i, which):
        return occupied.at[:, i, :, pl.ds(pl.multiple_of(which * LANES, LANES), LANES)]

    def field_copy(i):
        return remote(
            chunk(i, 1 - place), fields.at[place, i], field_send.at[i],
            field_recv.at[place, i], pair, o,
        )

    for i in range(band):
        field_copy(i).start()
    for i in range(band):
        pltpu.make_async_copy(
            chunk(i, place), fields.at[place, i], field_recv.at[place, i]
        ).start()

    lane = lax.broadcasted_iota(jnp.int32, (1, LANES), 1)
    cols = jnp.zeros((1, LANES), jnp.int32)
    for a in range(acols):
        cols = jnp.where(lane % acols == a, region_cols[a], cols)
    offset = lax.broadcasted_iota(jnp.int32, (width, LANES), 0) - cols + reach
    offset = jnp.where(offset < 0, offset + width, offset)
    offset = jnp.where(offset >= width, offset - width, offset)

    for d in range(1, 2 * reach):
        hot[d - 1] = jnp.where(offset == d, 1.0, 0.0).astype(jnp.bfloat16)

    for hop in range(1, row_count):
        for way in (1, -1):
            slot = (r + row_count - way * hop) % row_count
            follows = r + way
            here = r >= hop if way == 1 else r + hop < row_count

            @pl.when(here)
            def _():
                remote(
                    levels.at[slot], levels.at[slot], level_send.at[0, slot],
                    level_recv.at[slot], (r + row_count - way) % row_count, o,
                ).wait_recv()

                @pl.when((follows >= 0) & (follows < row_count))
                def _():
                    level_copy(slot, way).start()

    onsite = levels[0]
    for slot in range(1, row_count):
        onsite = onsite + levels[slot]
    onsite = onsite.astype(jnp.bfloat16)

    local_levels = {}
    for d in range(1, 2 * reach):
        here = jnp.dot(onsite, hot[d - 1], preferred_element_type=jnp.float32)
        local_levels[d] = jnp.concatenate([here, here], axis=1)

    lane = lax.broadcasted_iota(jnp.int32, (height, 2 * LANES), 1)
    row_id = lax.broadcasted_iota(jnp.int32, (height, 2 * LANES), 0)
    start = jnp.where(row_id == lane // acols, 1.0, 0.0)
    previous, current = {}, {reach: start}
    real = {reach: cheb_coef[0, 0] * start}
    imag = {reach: cheb_coef[1, 0] * start}
    for degree in range(1, terms):
        following = {}
        for d in range(reach - degree, reach + degree + 1):
            total = None
            if d in current:
                here = current[d]
                total = local_levels[d] * here - (
                    pltpu.roll(here, 1, 0) + pltpu.roll(here, height - 1, 0)
                )
            for beside in (d - 1, d + 1):
                if beside in current:
                    there = current[beside]
                    total = -there if total is None else total - there
            value = total * ((1.0 if degree == 1 else 2.0) / HOP_SCALE)
            if d in previous:
                value = value - previous[d]
            following[d] = value
            more_real = cheb_coef[0, degree] * value
            more_imag = cheb_coef[1, degree] * value
            real[d] = real[d] + more_real if d in real else more_real
            imag[d] = imag[d] + more_imag if d in imag else more_imag
        previous, current = current, following
    for d in range(2 * reach + 1):
        for part, parts in ((0, real), (1, imag)):
            for group in range(2):
                window[part, group, d] = parts[d][:, group * LANES : (group + 1) * LANES]

    depth = height // 2

    def expand(y, carry):
        for part in range(2):
            for group in range(2):
                dense = jnp.zeros((width, LANES), jnp.float32)
                for d in range(2 * reach + 1):
                    value = window[part, group, d, pl.ds(depth * side + y, 1), :]
                    dense = jnp.where(offset == d, value, dense)
                dense = dense.T
                high = dense.astype(jnp.bfloat16)
                low = (dense - high.astype(jnp.float32)).astype(jnp.bfloat16)
                sites = pl.ds((2 * part + group) * LANES, LANES)
                operator[0, y, sites, :] = high
                operator[1, y, sites, :] = low
        return carry

    lax.fori_loop(0, depth, expand, 0)

    for step in range(half):
        slot = (place + step) % half
        for i in range(band):
            remote(
                fields.at[slot, i], fields.at[slot, i], field_send.at[i],
                field_recv.at[slot, i], pair, o,
            ).wait_recv()
            both = jnp.concatenate([fields[slot, i, 0], fields[slot, i, 1]], axis=1)
            row = band * slot + i
            more = jnp.dot(
                operator[0, row], both, preferred_element_type=jnp.float32
            ) + jnp.dot(operator[1, row], both, preferred_element_type=jnp.float32)
            if step or i:
                more = product[...] + more
            product[...] = more
    for s in range(2):
        top = pl.ds(s * LANES, LANES)
        low = pl.ds((2 + s) * LANES, LANES)
        first, second = pl.ds(0, LANES), pl.ds(LANES, LANES)
        share0 = product[top, first] - product[low, second]
        share1 = product[top, second] + product[low, first]
        shares[s, 0] = share0
        shares[s, 1] = share1
        rounded[s, 0] = share0.astype(jnp.bfloat16)
        rounded[s, 1] = share1.astype(jnp.bfloat16)

    def base_copy():
        return remote(shares.at[1 - g], base, base_send, base_recv, r, mate)

    def cross_copy(s):
        return remote(
            rounded.at[s], crossed, cross_send.at[s], cross_recv, across, 2 * x + s
        )

    @pl.when(owner)
    def _():
        base_copy().start()
        pltpu.make_async_copy(shares.at[g], base, base_recv).start()

    @pl.when(jnp.logical_not(owner))
    def _():
        for s in range(2):
            cross_copy(s).start()

    base_copy().wait_recv()
    cross_copy(0).wait_recv()
    evolved[g] = (base[...] + crossed[...].astype(jnp.float32)).astype(jnp.bfloat16)

    def half_copy(slot):
        return remote(
            evolved.at[slot], evolved.at[slot], half_send, half_recv, r, mate
        )

    half_copy(g).start()
    half_copy(1 - g).wait_recv()

    left = jnp.concatenate(
        [jnp.concatenate([evolved[s, 0], evolved[s, 1]], axis=1) for s in range(2)], axis=0
    )
    columns = pl.ds(pl.multiple_of(g * tile, tile), tile)
    rights = []
    for s in range(2):
        p0 = evolved[s, 0, columns, :]
        p1 = evolved[s, 1, columns, :]
        rights.append(jnp.concatenate([p0, p1], axis=1))
        rights.append(jnp.concatenate([-p1, p0], axis=1))
    right = jnp.concatenate(rights, axis=0)
    blocks = lax.dot_general(
        left, right, (((1,), (1,)), ((), ())), preferred_element_type=jnp.float32
    )
    for s in range(2):
        for row in range(row_count):
            block = blocks[row * tile : (row + 1) * tile, s * LANES : (s + 1) * LANES]
            partial[2 * row + s] = block
            outgoing[2 * row + s] = block.astype(jnp.bfloat16)

    def block_copy(k, slot):
        to = (mine + k) % chips
        return remote(
            outgoing.at[to], incoming.at[slot], block_send.at[k - 1],
            block_recv.at[slot], to // 2, 2 * (to % 2) + g,
        )

    for k in range(1, chips):
        block_copy(k, mine).start()
    total = partial[mine]
    for k in range(1, chips):
        slot = (mine + chips - k) % chips
        block_copy(k, slot).wait_recv()
        total = total + incoming[slot].astype(jnp.float32)
    out[0] = prior[0].astype(jnp.float32) + total[:, :tile]
    out[1] = prior[1].astype(jnp.float32) + total[:, tile:]

    for hop in range(row_count):
        for way in (1, -1):
            slot = (r + row_count - way * hop) % row_count
            follows = r + way
            here = r >= hop if way == 1 else r + hop < row_count

            @pl.when(here & (follows >= 0) & (follows < row_count))
            def _():
                level_copy(slot, way).wait_send()

    for i in range(band):
        field_copy(i).wait_send()
    pl.when(owner)(lambda: base_copy().wait_send())

    @pl.when(jnp.logical_not(owner))
    def _():
        for s in range(2):
            cross_copy(s).wait_send()

    half_copy(g).wait_send()
    for k in range(1, chips):
        block_copy(k, mine).wait_send()


def fused_step(row_count, occupied, disorder, region_cols, cheb_coef, prior_corr):
    band, width = disorder.shape
    terms = cheb_coef.shape[1]
    tile = prior_corr.shape[1]
    height = band * row_count
    chips = 2 * row_count
    half = row_count // 2
    dma = pltpu.SemaphoreType.DMA
    vmem = pl.BlockSpec(memory_space=pltpu.VMEM)
    smem = pl.BlockSpec(memory_space=pltpu.SMEM)
    return pl.pallas_call(
        functools.partial(quench_kernel, row_count),
        out_shape=jax.ShapeDtypeStruct(prior_corr.shape, jnp.float32),
        in_specs=[pl.BlockSpec(memory_space=pl.ANY), vmem, smem, smem, vmem],
        out_specs=vmem,
        scratch_shapes=[
            pltpu.VMEM((half, band, 2, width, LANES), jnp.bfloat16),
            pltpu.VMEM((row_count, height, width), jnp.float32),
            pltpu.VMEM((2 * terms - 3, width, LANES), jnp.bfloat16),
            pltpu.VMEM((2, 2, 2 * terms - 1, height, LANES), jnp.float32),
            pltpu.VMEM((2, height // 2, 4 * LANES, width), jnp.bfloat16),
            pltpu.VMEM((4 * LANES, 2 * LANES), jnp.float32),
            pltpu.VMEM((2, 2, LANES, LANES), jnp.float32),
            pltpu.VMEM((2, 2, LANES, LANES), jnp.bfloat16),
            pltpu.VMEM((2, LANES, LANES), jnp.float32),
            pltpu.VMEM((2, LANES, LANES), jnp.bfloat16),
            pltpu.VMEM((2, 2, LANES, LANES), jnp.bfloat16),
            pltpu.VMEM((chips, tile, LANES), jnp.float32),
            pltpu.VMEM((chips, tile, LANES), jnp.bfloat16),
            pltpu.VMEM((chips, tile, LANES), jnp.bfloat16),
            dma((2, row_count)),
            dma((row_count,)),
            dma((band,)),
            dma((half, band)),
            dma,
            dma,
            dma((2,)),
            dma,
            dma,
            dma,
            dma((chips - 1,)),
            dma((chips,)),
        ],
        compiler_params=pltpu.CompilerParams(collective_id=0, has_side_effects=True),
    )(occupied, disorder, region_cols, cheb_coef, prior_corr)


def local_step(row_count, orb_count, occupied, disorder, region_cols, cheb_coef, prior_corr):
    band, width, orbitals = occupied.shape[1:]
    terms = cheb_coef.shape[1]
    height = band * row_count
    sites = height * region_cols.shape[0]
    fused = (
        orb_count == 4
        and sites == 2 * LANES
        and 2 * orbitals == row_count * LANES
        and orbitals == 2 * LANES
        and height % 8 == 0
        and width % LANES == 0
        and width >= 2 * terms
        and LANES % region_cols.shape[0] == 0
        and prior_corr.shape[1:] == (LANES // 2, LANES // 2)
    )
    if fused:
        return fused_step(row_count, occupied, disorder, region_cols, cheb_coef, prior_corr)
    return shards(occupied, disorder, region_cols, cheb_coef, prior_corr)


def solution(mesh):
    return jax.shard_map(
        functools.partial(local_step, mesh.shape["rows"], mesh.shape["orb"]),
        mesh=mesh,
        in_specs=(
            P(None, ("real", "rows"), None, "orb"),
            P(("real", "rows"), None),
            P(),
            P(),
            P(None, ("real", "rows"), "orb"),
        ),
        out_specs=P(None, ("real", "rows"), "orb"),
        check_vma=False,
    )
```
